128 devices in a mesh: gx: 16 (over x_lo, z, core), gy: 8 (over x_hi, y).
Axes of the slice: x: 4 (x_hi: 2, x_lo: 2; x = x_hi * 2 + x_lo), y: 4, z: 4, core: 2. Of those that a mesh axis runs over, the one named last changes fastest.
Arguments:
- velocity: float32 [3, 512, 512, 128], P(None, 'gx', 'gy'), may hold values from -6 to 6
- stress: float32 [6, 512, 512, 128], P(None, 'gx', 'gy'), may hold values from -9 to 9
- material: float32 [3, 512, 512, 128], P(None, 'gx', 'gy'), may hold values from 0.3 to 1
- src_x: int32 [2, 64], replicated, may hold values from 0 to 511
- src_y: int32 [2, 64], replicated, may hold values from 0 to 511
- src_amp: float32 [2, 64], replicated, may hold values from -30 to 30
- chan_block: int32 [32768, 1], P(('gx', 'gy')), may hold values from 0 to 127; in each aligned block of 256 rows (0 to 255, 256 to 511, ...) at most 4 rows name the same one
- chan_cell: int32 [32768], P(('gx', 'gy')), may hold values from 0 to 262143
- chan_azimuth: float32 [32768], P(('gx', 'gy')), may hold values from -3.140625 to 3.140625
- gauge: int32 [32768], P(('gx', 'gy')), may hold values from 2 to 16
Outputs:
- velocity_out: float32 [3, 512, 512, 128], P(None, 'gx', 'gy')
- stress_out: float32 [6, 512, 512, 128], P(None, 'gx', 'gy')
- strain_rate: float32 [32768], P(('gx', 'gy'))
The draws below stay inside these ranges and needn't reach their ends.
Inputs may be any that keep to these rules, and one draw needn't show every extreme that they name: `chan_block`: among the 256 channels of one fibre segment (the channels of one device) no grid block is named more than 4 times, and in every draw some grid block is named exactly 4 times by some segment.
All inputs are finite; a program needn't handle non-finite values.
Results may differ from the reference program's by a relative error of at most 0.00012.
Values sent between devices are 32-bit elements; how exact they have to be, the bound alone decides.
No kernel may reach another device: no remote copies, remote signals or barrier semaphores. Data moves between devices by JAX's collectives and lax.ppermute only.
A program may use at most 128 MiB of HBM per device.

```python
import math
import jax
import jax.numpy as jnp
import numpy as np
from jax import lax

CX = 32
CY = 64
NZ = 128
STEPS = 2
NSRC = 64
CH_DEV = 256
NX = 512
NY = 512
CH = 32768
CAP = 4
N_GX = 16
N_GY = 8


def draw_stress(key, part):
    rough_key = jax.random.fold_in(key, 11)
    count_key = jax.random.fold_in(key, 12)
    sign_key = jax.random.fold_in(key, 13)
    phase_key = jax.random.fold_in(key, 14)
    rough = jnp.clip(jax.random.normal(rough_key, (6, NX, NY, NZ), jnp.float32), -5.0, 5.0)
    height = 4.0
    counts = jax.random.randint(count_key, (6, 3), 7, 12)
    signs = jax.random.randint(sign_key, (6, 3), 0, 2) * 2 - 1
    waves = (counts * signs).astype(jnp.int32)
    phases = jax.random.uniform(phase_key, (6,), jnp.float32, 0.0, 2.0 * math.pi)
    pos_x = jnp.arange(NX, dtype=jnp.int32)
    pos_y = jnp.arange(NY, dtype=jnp.int32)
    pos_z = jnp.arange(NZ, dtype=jnp.int32)
    index = (waves[:, 0, None, None, None] * pos_x[None, :, None, None] + waves[:, 1, None, None, None] * pos_y[None, None, :, None] + waves[:, 2, None, None, None] * pos_z[None, None, None, :]) % 128
    angle = index.astype(jnp.float32) * (2.0 * math.pi / 128.0) + phases[:, None, None, None]
    return rough + height * jnp.cos(angle)


def plant(drawn, own_key, smallest, high):
    spot = [jax.random.randint(jax.random.fold_in(own_key, axis), (), 0, length) for axis, length in enumerate(drawn.shape)]
    widest = drawn.shape.index(max(drawn.shape))
    beside = spot[:widest] + [(spot[widest] + 1) % drawn.shape[widest]] + spot[widest + 1:]
    return drawn.at[tuple(spot)].set(smallest).at[tuple(beside)].set(high)


def levels(own_key, shape, shards, least, top_value):
    factor_of, own = 1.0, jax.random.fold_in(own_key, 6)
    for position, shards_of in shards:
        heights = jnp.exp(jax.random.uniform(jax.random.fold_in(own, position), (shards_of,), jnp.float32, least / len(shards), top_value / len(shards)))
        factor_of = factor_of * jnp.repeat(heights, shape[position] // shards_of).reshape([-1 if axis == position else 1 for axis in range(len(shape))])
    return factor_of


def shared_out(rng, own, number, rows, count, top, limit, lean):
    ranking = jax.random.permutation(rng, count)
    heavy_load, ordinary = load_shares(count, rows * top, limit, lean, True), load_shares(count, rows * top, limit, lean, False)
    places = jnp.arange(count)

    def named(sizes, turn):
        used = int((sizes > 0).sum())
        fixed = max(1, used // 4)
        passed = fixed + (places - fixed + turn * (used - fixed)) % max(1, count - fixed)
        return jnp.zeros((count,), jnp.int32).at[ranking[jnp.where(places < fixed, places, passed)]].set(jnp.asarray(sizes, jnp.int32))

    sizes = jnp.where(number % 4 == 0, named(heavy_load, number // 4), named(ordinary, number - number // 4 - 1))
    mixed = jax.random.permutation(jax.random.fold_in(own, 3), count)
    donor, taker = mixed[0:count // 2 * 2:2], mixed[1:count // 2 * 2:2]
    slack = jnp.minimum(sizes[donor] - 1, limit - sizes[taker]) // 2
    slack = jnp.where((donor == ranking[0]) | (taker == ranking[0]) | (sizes[taker] == 0), 0, jnp.maximum(slack, 0))
    passed = jax.random.randint(jax.random.fold_in(own, 4), (count // 2,), 0, 1 << 20) % (slack + 1)
    sizes = sizes.at[donor].add(-passed).at[taker].add(passed)
    labels = jnp.searchsorted(jnp.cumsum(sizes), jnp.arange(rows * top), side="right").astype(jnp.int32)
    table = labels.reshape(top, rows).T
    table = table[jax.random.permutation(jax.random.fold_in(own, 1), rows)]
    turn = jax.random.randint(jax.random.fold_in(own, 2), (rows, 1), 0, top)
    return jnp.take_along_axis(table, (jnp.arange(top)[None, :] + turn) % top, axis=1)


def load_shares(number_of, total, limit, lean, full):
    loads = [(1 << 20) // math.isqrt(grade ** lean) + 1 for grade in range(1, number_of + 1)]
    largest = limit if full else min(limit, max(-(-total // number_of), total * loads[0] // sum(loads)))
    least = 1 if total - largest >= number_of - 1 else 0
    given, rest = [largest] + [least] * (number_of - 1), total - largest - least * (number_of - 1)
    while rest > 0:
        candidates = [i for i in range(1, number_of) if given[i] < largest] or [i for i in range(1, number_of) if given[i] < limit]
        pool, left = sum([loads[i] for i in candidates]), rest
        for i in candidates:
            addition = min(limit - given[i], max(1, left * loads[i] // pool), rest)
            given[i] = given[i] + addition
            rest = rest - addition
    return np.array(given)


def normal_values(key, dims, width, reach, split=(), held_as=jnp.bfloat16):
    entries = width * jax.random.normal(key, dims, jnp.float32)
    if split:
        entries = entries * levels(key, dims, split, -0.22, 0.18)
    return jnp.clip(entries, -reach, reach).astype(held_as)


def setup_inputs(seed: int = 0) -> dict:
    key_list = jax.random.split(jax.random.key(seed), 11)
    velocity = normal_values(key_list[0], (3, NX, NY, NZ), 1.0, 6.0, ((1, 16), (2, 8)), jnp.float32)
    stress = draw_stress(jax.random.fold_in(key_list[10], 71), 0)
    material = jnp.clip(jnp.exp(math.log(1.0) - 1.2039728 * jax.random.uniform(key_list[2], (3, NX, NY, NZ), jnp.float32) ** levels(key_list[2], (3, NX, NY, NZ), ((1, 16), (2, 8)), -0.2, 0.2)), 0.3, 1.0)
    src_x = plant(jax.random.randint(key_list[3], (STEPS, NSRC), 0, NX), jax.random.fold_in(key_list[3], 1), 0, NX - 1).astype(jnp.int32)
    src_y = plant(jax.random.randint(key_list[4], (STEPS, NSRC), 0, NY), jax.random.fold_in(key_list[4], 1), 0, NY - 1).astype(jnp.int32)
    src_amp = normal_values(key_list[5], (STEPS, NSRC), 5.0, 30.0, (), jnp.float32)
    chan_block_keys = jax.random.split(jax.random.fold_in(key_list[6], 1), CH // CH_DEV)
    chan_block_turns = jax.random.permutation(jax.random.fold_in(key_list[6], 3), CH // CH_DEV)
    chan_block = jax.vmap(lambda own, number: shared_out(jax.random.fold_in(key_list[6], 2), own, number, CH_DEV, N_GX * N_GY, 1, CAP, 2))(chan_block_keys, chan_block_turns).reshape((CH, 1))
    chan_cell = plant(jax.random.randint(key_list[7], (CH,), 0, CX * CY * NZ), jax.random.fold_in(key_list[7], 1), 0, (CX * CY * NZ) - 1).astype(jnp.int32)
    chan_azimuth = jnp.clip(jax.random.uniform(key_list[8], (CH,), jnp.float32, -3.140625, 3.140625), -3.140625, 3.140625)
    gauge = plant(jax.random.randint(key_list[9], (CH,), 2, 17), jax.random.fold_in(key_list[9], 1), 2, 16).astype(jnp.int32)
    return {"velocity": velocity, "stress": stress, "material": material, "src_x": src_x, "src_y": src_y, "src_amp": src_amp, "chan_block": chan_block, "chan_cell": chan_cell, "chan_azimuth": chan_azimuth, "gauge": gauge}


COEFFS = (1225.0 / 1024.0, -245.0 / 3072.0, 49.0 / 5120.0, -5.0 / 7168.0)
time_step = 0.2


def padded(field, axis):
    widths = [(0, 0)] * field.ndim
    widths[axis] = (4, 4)
    return jnp.pad(field, widths)


def forward_diff(extended, axis, length):
    total = 0.0
    for order in range(1, 5):
        ahead = lax.slice_in_dim(extended, 4 + order, 4 + order + length, axis=axis)
        behind = lax.slice_in_dim(extended, 5 - order, 5 - order + length, axis=axis)
        total = total + COEFFS[order - 1] * (ahead - behind)
    return total


def backward_diff(extended, axis, length):
    total = 0.0
    for order in range(1, 5):
        ahead = lax.slice_in_dim(extended, 3 + order, 3 + order + length, axis=axis)
        behind = lax.slice_in_dim(extended, 4 - order, 4 - order + length, axis=axis)
        total = total + COEFFS[order - 1] * (ahead - behind)
    return total


def update_velocity(velocity, stress, buoyancy, force, x_ext, y_ext):
    count_x, count_y, depth = buoyancy.shape
    rate_x = forward_diff(x_ext[0], 0, count_x) + backward_diff(y_ext[0], 1, count_y) + backward_diff(padded(stress[1], 2), 2, depth)
    rate_y = backward_diff(x_ext[2], 0, count_x) + forward_diff(y_ext[2], 1, count_y) + backward_diff(padded(stress[3], 2), 2, depth)
    rate_z = backward_diff(x_ext[1], 0, count_x) + backward_diff(y_ext[1], 1, count_y) + forward_diff(padded(stress[5], 2), 2, depth)
    rate_z = rate_z.at[:, :, 0].add(force)
    return jnp.stack([velocity[0] + time_step * buoyancy * rate_x,
                      velocity[1] + time_step * buoyancy * rate_y,
                      velocity[2] + time_step * buoyancy * rate_z])


def update_stress(velocity, stress, lame, shear, vel_x_ext, vel_y_ext):
    count_x, count_y, depth = lame.shape
    strain_xx = backward_diff(vel_x_ext[0], 0, count_x)
    strain_yy = backward_diff(vel_y_ext[1], 1, count_y)
    strain_zz = backward_diff(padded(velocity[2], 2), 2, depth)
    trace_sum = strain_xx + strain_yy + strain_zz
    shear_xy = forward_diff(vel_y_ext[0], 1, count_y) + forward_diff(vel_x_ext[1], 0, count_x)
    shear_xz = forward_diff(padded(velocity[0], 2), 2, depth) + forward_diff(vel_x_ext[2], 0, count_x)
    shear_yz = forward_diff(padded(velocity[1], 2), 2, depth) + forward_diff(vel_y_ext[2], 1, count_y)
    return jnp.stack([stress[0] + time_step * (lame * trace_sum + 2.0 * shear * strain_xx),
                      stress[1] + time_step * shear * shear_xz,
                      stress[2] + time_step * shear * shear_xy,
                      stress[3] + time_step * shear * shear_yz,
                      stress[4] + time_step * (lame * trace_sum + 2.0 * shear * strain_yy),
                      stress[5] + time_step * (lame * trace_sum + 2.0 * shear * strain_zz)])


def reference(velocity, stress, material, src_x, src_y, src_amp, chan_block, chan_cell, chan_azimuth, gauge):
    lame, shear, buoyancy = material[0], material[1], material[2]
    for step in range(STEPS):
        force = jnp.zeros((NX, NY), jnp.float32).at[src_x[step], src_y[step]].add(src_amp[step])
        velocity = update_velocity(velocity, stress, buoyancy, force, padded(stress[0:3], 1), padded(stress[2:5], 2))
        stress = update_stress(velocity, stress, lame, shear, padded(velocity, 1), padded(velocity, 2))
    block = chan_block[:, 0]
    cell_x = (block // N_GY) * CX + chan_cell // (CY * NZ)
    cell_y = (block % N_GY) * CY + (chan_cell // NZ) % CY
    cell_z = chan_cell % NZ
    along = jnp.cos(chan_azimuth) * velocity[0][cell_x, cell_y, cell_z] + jnp.sin(chan_azimuth) * velocity[1][cell_x, cell_y, cell_z]
    joined = jnp.concatenate([along, jnp.zeros_like(along)])
    positions = jnp.arange(CH, dtype=jnp.int32) + gauge.astype(jnp.int32)
    ahead = jnp.take(joined, positions)
    strain = (ahead - along) / gauge.astype(jnp.float32)
    return velocity, stress, strain
```

```python
import jax
import jax.numpy as jnp
import numpy as np
from jax import lax
from jax.experimental import pallas as pl
from jax.experimental.pallas import tpu as pltpu
from jax.sharding import PartitionSpec as P

STEPS = 2
COEFFS = (1225.0 / 1024.0, -245.0 / 3072.0, 49.0 / 5120.0, -5.0 / 7168.0)
RATIO = tuple(c / COEFFS[0] for c in COEFFS)
time_step = 0.2
SCALE = time_step * COEFFS[0]
R = 4
OX, OY = 4, 8
PLANES = 2

VM = pl.BlockSpec(memory_space=pltpu.VMEM)
SM = pl.BlockSpec(memory_space=pltpu.SMEM)
HB = pl.BlockSpec(memory_space=pltpu.HBM)
F32 = jnp.float32
BF16 = jnp.bfloat16


def shape(*dims):
    return jax.ShapeDtypeStruct(dims, F32)


def swap_pairs(count, first):
    route = []
    for i in range(first, count - 1, 2):
        route += [(i, i + 1), (i + 1, i)]
    return route


def depth_table(depth, forward):
    table = np.zeros((depth, depth), np.float64)
    for m in range(1, 5):
        up, down = (m, 1 - m) if forward else (m - 1, -m)
        for t in range(depth):
            if 0 <= t + up < depth:
                table[t + up, t] += RATIO[m - 1]
            if 0 <= t + down < depth:
                table[t + down, t] -= RATIO[m - 1]
    high = jnp.asarray(table, F32).astype(BF16)
    low = (jnp.asarray(table, F32) - high.astype(F32)).astype(BF16)
    row = jnp.concatenate([high, low], axis=1)
    return jnp.concatenate([row, row], axis=0)


def diff_x(ref, f, x, r0, n, forward):
    total = None
    for m in range(1, 5):
        up, down = (m, 1 - m) if forward else (m - 1, -m)
        term = ref[f, x + OX + up, OY + r0 : OY + r0 + n, :] - ref[f, x + OX + down, OY + r0 : OY + r0 + n, :]
        total = term if m == 1 else total + RATIO[m - 1] * term
    return total


def diff_y(ref, f, x, r0, n, forward):
    total = None
    for m in range(1, 5):
        up, down = (m, 1 - m) if forward else (m - 1, -m)
        a, b = OY + r0 + up, OY + r0 + down
        term = ref[f, x + OX, a : a + n, :] - ref[f, x + OX, b : b + n, :]
        total = term if m == 1 else total + RATIO[m - 1] * term
    return total


def diff_z(ref, fields, x, planes, ny, table):
    parts = []
    for f in fields:
        for p in range(planes):
            v = ref[f, x + p + OX, OY : OY + ny, :]
            high = v.astype(BF16)
            low = (v - high.astype(F32)).astype(BF16)
            parts.append(jnp.concatenate([high, low], axis=1))
    both = jnp.dot(jnp.concatenate(parts, axis=0), table, preferred_element_type=F32)
    depth = both.shape[1] // 2
    return both[:, :depth] + both[:, depth:]


def put_halos(ext, xf, yf, px, py, rxe, rxo, rye, ryo):
    nx, ny = ext.shape[1] - 2 * OX, ext.shape[2] - 2 * OY
    e, o = (OX + nx) * (1 - px), (OX + nx) * px
    for i, f in enumerate(xf):
        ext[f, pl.ds(e, R), OY : OY + ny, :] = rxe[i]
        ext[f, pl.ds(o, R), OY : OY + ny, :] = rxo[i]

    def rows(at_e, at_o):
        def step(x, carry):
            for i, f in enumerate(yf):
                ext[f, x + OX, at_e : at_e + R, :] = rye[i, x]
                ext[f, x + OX, at_o : at_o + R, :] = ryo[i, x]
            return carry

        lax.fori_loop(0, nx, step, 0)

    pl.when(py == 0)(lambda: rows(OY + ny, OY - R))
    pl.when(py == 1)(lambda: rows(OY - R, OY + ny))


def take_edges(ext, xf, yf, px, py, sxe, sxo, sye, syo):
    nx, ny = ext.shape[1] - 2 * OX, ext.shape[2] - 2 * OY
    e, o = OX + (nx - R) * (1 - px), OX + (nx - R) * px
    for i, f in enumerate(xf):
        sxe[i] = ext[f, pl.ds(e, R), OY : OY + ny, :]
        sxo[i] = ext[f, pl.ds(o, R), OY : OY + ny, :]

    def rows(at_e, at_o):
        def step(x, carry):
            for i, f in enumerate(yf):
                sye[i, x] = ext[f, x + OX, at_e : at_e + R, :]
                syo[i, x] = ext[f, x + OX, at_o : at_o + R, :]
            return carry

        lax.fori_loop(0, nx, step, 0)

    pl.when(py == 0)(lambda: rows(OY + ny - R, OY))
    pl.when(py == 1)(lambda: rows(OY, OY + ny - R))


def pack_kernel(place, stress, sxe, sxo, sye, syo, tile_e, tile_o, sems):
    nx, ny = stress.shape[1], stress.shape[2]
    px, py = place[0] % 2, place[1] % 2
    e, o = (nx - R) * (1 - px), (nx - R) * px
    te, to = pl.multiple_of((ny - 8) * (1 - py), 8), pl.multiple_of((ny - 8) * py, 8)
    copies = [
        pltpu.make_async_copy(stress.at[2:5, :, pl.ds(te, 8), :], tile_e, sems.at[0]),
        pltpu.make_async_copy(stress.at[2:5, :, pl.ds(to, 8), :], tile_o, sems.at[1]),
        pltpu.make_async_copy(stress.at[0:3, pl.ds(e, R)], sxe, sems.at[2]),
        pltpu.make_async_copy(stress.at[0:3, pl.ds(o, R)], sxo, sems.at[3]),
    ]
    for c in copies:
        c.start()
    copies[0].wait()
    copies[1].wait()

    def rows(at_e, at_o):
        def step(x, carry):
            for i in range(3):
                sye[i, x] = tile_e[i, x, at_e : at_e + R, :]
                syo[i, x] = tile_o[i, x, at_o : at_o + R, :]
            return carry

        lax.fori_loop(0, nx, step, 0)

    pl.when(py == 0)(lambda: rows(8 - R, 0))
    pl.when(py == 1)(lambda: rows(0, 8 - R))
    copies[2].wait()
    copies[3].wait()


def velocity_kernel(step, first, *refs):
    if first:
        (place, sx, sy, amp, stress, vel, mat, tm, tp, rxe, rxo, rye, ryo,
         ve, se, sxe, sxo, sye, syo, sems) = refs
        nx, ny = stress.shape[1], stress.shape[2]
        loads = [
            pltpu.make_async_copy(stress, se.at[:, OX : OX + nx, OY : OY + ny, :], sems.at[0]),
            pltpu.make_async_copy(vel, ve.at[:, OX : OX + nx, OY : OY + ny, :], sems.at[1]),
        ]
        for c in loads:
            c.start()
    else:
        (place, sx, sy, amp, _, _, mat, tm, tp, rxe, rxo, rye, ryo,
         ve, se, sxe, sxo, sye, syo) = refs
    nx, ny = se.shape[1] - 2 * OX, se.shape[2] - 2 * OY
    px, py = place[0] % 2, place[1] % 2
    put_halos(se, (0, 1, 2), (2, 3, 4), px, py, rxe, rxo, rye, ryo)
    if first:
        for c in loads:
            c.wait()

    def advance(it, carry):
        x0 = it * PLANES
        zm = diff_z(se, (1, 3), x0, PLANES, ny, tm[...])
        zp = diff_z(se, (5,), x0, PLANES, ny, tp[...])
        n = 16
        for p in range(PLANES):
            x = x0 + p
            for r0 in range(0, ny, n):
                a, b = p * ny + r0, (PLANES + p) * ny + r0
                here = (slice(OY + r0, OY + r0 + n), slice(None))
                sb = SCALE * mat[2, x, r0 : r0 + n, :]
                rate = diff_x(se, 0, x, r0, n, True) + diff_y(se, 2, x, r0, n, False) + zm[a : a + n]
                ve[(0, x + OX, *here)] = ve[(0, x + OX, *here)] + sb * rate
                rate = diff_x(se, 2, x, r0, n, False) + diff_y(se, 4, x, r0, n, True) + zm[b : b + n]
                ve[(1, x + OX, *here)] = ve[(1, x + OX, *here)] + sb * rate
                rate = diff_x(se, 1, x, r0, n, False) + diff_y(se, 3, x, r0, n, False) + zp[a : a + n]
                ve[(2, x + OX, *here)] = ve[(2, x + OX, *here)] + sb * rate
        return carry

    lax.fori_loop(0, nx // PLANES, advance, 0)

    surface = lax.broadcasted_iota(jnp.int32, (1, se.shape[3]), 1) == 0

    def load(k, carry):
        x, y = sx[step, k] - place[0] * nx, sy[step, k] - place[1] * ny

        @pl.when((x >= 0) & (x < nx) & (y >= 0) & (y < ny))
        def _():
            row = (2, x + OX, pl.ds(y + OY, 1), slice(None))
            push = (time_step * amp[step, k]) * mat[2, x, pl.ds(y, 1), :]
            ve[row] = ve[row] + jnp.where(surface, push, 0.0)

        return carry

    lax.fori_loop(0, sx.shape[1], load, 0)
    take_edges(ve, (0, 1, 2), (0, 1, 2), px, py, sxe, sxo, sye, syo)


def stress_kernel(last, *refs):
    if last:
        (place, _, se, mat, tm, tp, rxe, rxo, rye, ryo, ve, vout, sout, snew, sems) = refs
        nx, ny = ve.shape[1] - 2 * OX, ve.shape[2] - 2 * OY
        inner = (slice(None), slice(OX, OX + nx), slice(OY, OY + ny), slice(None))
        vcopy = pltpu.make_async_copy(ve.at[inner], vout, sems.at[0])
        vcopy.start()
    else:
        (place, _, _, mat, tm, tp, rxe, rxo, rye, ryo, ve, se, sxe, sxo, sye, syo) = refs
        snew = se
    nx, ny = ve.shape[1] - 2 * OX, ve.shape[2] - 2 * OY
    px, py = place[0] % 2, place[1] % 2
    put_halos(ve, (0, 1, 2), (0, 1, 2), px, py, rxe, rxo, rye, ryo)
    ox, oy = (0, 0) if last else (OX, OY)

    def advance(it, carry):
        x0 = it * PLANES
        zp = diff_z(ve, (0, 1), x0, PLANES, ny, tp[...])
        zm = diff_z(ve, (2,), x0, PLANES, ny, tm[...])
        n = 16
        for p in range(PLANES):
            x = x0 + p
            for r0 in range(0, ny, n):
                a, b = p * ny + r0, (PLANES + p) * ny + r0

                def add(f, change):
                    snew[f, x + ox, oy + r0 : oy + r0 + n, :] = (
                        se[f, x + OX, OY + r0 : OY + r0 + n, :] + change
                    )

                exx = diff_x(ve, 0, x, r0, n, False)
                eyy = diff_y(ve, 1, x, r0, n, False)
                ezz = zm[a : a + n]
                trace = (SCALE * mat[0, x, r0 : r0 + n, :]) * (exx + eyy + ezz)
                smu = SCALE * mat[1, x, r0 : r0 + n, :]
                add(0, trace + (2.0 * smu) * exx)
                add(4, trace + (2.0 * smu) * eyy)
                add(5, trace + (2.0 * smu) * ezz)
                add(2, smu * (diff_y(ve, 0, x, r0, n, True) + diff_x(ve, 1, x, r0, n, True)))
                add(1, smu * (zp[a : a + n] + diff_x(ve, 2, x, r0, n, True)))
                add(3, smu * (zp[b : b + n] + diff_y(ve, 2, x, r0, n, True)))
        if last:
            at = pl.ds(x0, PLANES)
            pltpu.make_async_copy(snew.at[:, at], sout.at[:, at], sems.at[1]).start()
        return carry

    lax.fori_loop(0, nx // PLANES, advance, 0)
    if last:
        pltpu.make_async_copy(snew, sout, sems.at[1]).wait()
        vcopy.wait()
    else:
        take_edges(se, (0, 1, 2), (2, 3, 4), px, py, sxe, sxo, sye, syo)


def to_column(row, i, width):
    eye = lax.broadcasted_iota(jnp.int32, (width, width), 0) == lax.broadcasted_iota(
        jnp.int32, (width, width), 1
    )
    part = jnp.broadcast_to(row[:, i * width : (i + 1) * width], (width, width))
    return jnp.sum(jnp.where(eye, part, 0.0), axis=1, keepdims=True)


def ranks(block):
    count = block.shape[1]
    later = lax.broadcasted_iota(jnp.int32, (128, count), 1)
    total = jnp.zeros((1, count), F32)
    for i in range(count // 128):
        earlier = lax.broadcasted_iota(jnp.int32, (128, count), 0) + i * 128
        same = (to_column(block, i, 128) == block) & (earlier < later)
        total = total + jnp.sum(jnp.where(same, 1.0, 0.0), axis=0, keepdims=True)
    return total


def members(block, devices):
    owner = lax.broadcasted_iota(jnp.int32, (devices, block.shape[1]), 0).astype(F32)
    return jnp.where(owner == block, 1.0, 0.0)


def request_kernel(block_ref, cell_ref, cos_ref, sin_ref, out):
    devices, slots = out.shape[0], out.shape[1] // 4
    block = block_ref[...].astype(F32)
    rank = ranks(block)
    place = lax.broadcasted_iota(jnp.int32, block.shape, 1).astype(F32) + 1.0
    rows = []
    for value in (cell_ref[...].astype(F32) + 1.0, cos_ref[...], sin_ref[...], place):
        for r in range(slots):
            rows.append(jnp.where(rank == float(r), value, 0.0))
    out[...] = lax.dot_general(
        members(block, devices),
        jnp.concatenate(rows, axis=0),
        (((1,), (1,)), ((), ())),
        precision=lax.Precision.HIGHEST,
        preferred_element_type=F32,
    )


def pick_kernel(want, asked, ve, out, rows_x, rows_y, ahead):
    devices, slots = asked.shape[0], asked.shape[1] // 4
    ny, depth = ve.shape[2] - 2 * OY, ve.shape[3]

    def fetch(s, carry):
        for r in range(slots):
            cell = jnp.maximum(want[s, r].astype(jnp.int32) - 1, 0)
            x = cell // (ny * depth)
            y = (cell // depth) % ny
            rows_x[r, pl.ds(s, 1), :] = ve[0, x + OX, pl.ds(y + OY, 1), :]
            rows_y[r, pl.ds(s, 1), :] = ve[1, x + OX, pl.ds(y + OY, 1), :]
        return carry

    lax.fori_loop(0, devices, fetch, 0)
    asks = asked[...]
    lane = lax.broadcasted_iota(jnp.int32, (devices, depth), 1)
    column = lax.broadcasted_iota(jnp.int32, asks.shape, 1)
    picked = jnp.zeros(asks.shape, F32)
    for r in range(slots):
        cell = asks[:, r : r + 1].astype(jnp.int32) - 1
        hit = (cell >= 0) & (lane == cell % depth)
        along = asks[:, slots + r : slots + r + 1] * rows_x[r] + asks[:, 2 * slots + r : 2 * slots + r + 1] * rows_y[r]
        value = jnp.sum(jnp.where(hit, along, 0.0), axis=1, keepdims=True)
        picked = jnp.where(column == r, value, picked)
    ahead[devices : devices + 8, :] = jnp.zeros((8, asks.shape[1]), F32)
    ahead[0:devices, :] = jnp.where(column >= 3 * slots, asks, picked)
    nxt = ahead[1 : devices + 1, :]
    out[...] = jnp.where(column < slots, picked, jnp.where(column >= 3 * slots, nxt, pltpu.roll(nxt, slots, 1)))


def strain_kernel(block_ref, gauge_ref, back_ref, out):
    devices, slots = back_ref.shape[0], back_ref.shape[1] // 4
    count = block_ref.shape[1]
    block, gauge = block_ref[...].astype(F32), gauge_ref[...]
    back = back_ref[...]
    rank = ranks(block)
    mine = lax.dot_general(
        back,
        members(block, devices),
        (((0,), (0,)), ((), ())),
        precision=lax.Precision.HIGHEST,
        preferred_element_type=F32,
    )
    along = jnp.zeros((1, count), F32)
    for r in range(slots):
        along = along + jnp.where(rank == float(r), mine[r : r + 1, :], 0.0)
    place = lax.broadcasted_iota(jnp.int32, (devices, 128), 1).astype(F32) + 1.0
    following = jnp.zeros((1, 128), F32)
    for r in range(slots):
        hit = back[:, 3 * slots + r : 3 * slots + r + 1] == place
        following = following + jnp.sum(
            jnp.where(hit, back[:, slots + r : slots + r + 1], 0.0), axis=0, keepdims=True
        )
    goal = lax.broadcasted_iota(jnp.int32, (128, count), 1) + gauge
    ahead = jnp.zeros((1, count), F32)
    for i in range(count // 128 + 1):
        values = to_column(along, i, 128) if i < count // 128 else to_column(following, 0, 128)
        source = lax.broadcasted_iota(jnp.int32, (128, count), 0) + i * 128
        ahead = ahead + jnp.sum(jnp.where(source == goal, values, 0.0), axis=0, keepdims=True)
    out[...] = (ahead - along) / gauge.astype(F32)


def call(kernel, outs, in_specs, out_specs, scratch=(), aliases=None, cost=None, mib=8):
    return pl.pallas_call(
        kernel,
        out_shape=outs,
        in_specs=in_specs,
        out_specs=out_specs,
        scratch_shapes=list(scratch),
        input_output_aliases=aliases or {},
        compiler_params=pltpu.CompilerParams(vmem_limit_bytes=mib << 20),
        cost_estimate=cost,
    )


def exchange(edges):
    sxe, sxo, sye, syo = edges
    ngx, ngy = lax.axis_size("gx"), lax.axis_size("gy")
    ryo = lax.ppermute(syo, "gy", swap_pairs(ngy, 1))
    rxo = lax.ppermute(sxo, "gx", swap_pairs(ngx, 1))
    rye = lax.ppermute(sye, "gy", swap_pairs(ngy, 0))
    rxe = lax.ppermute(sxe, "gx", swap_pairs(ngx, 0))
    return rxe, rxo, rye, ryo


def body(velocity, stress, material, src_x, src_y, src_amp, chan_block, chan_cell, chan_azimuth, gauge):
    _, nx, ny, nz = material.shape
    devices = lax.axis_size("gx") * lax.axis_size("gy")
    count = chan_cell.shape[0]
    slots = 4
    place = jnp.stack([lax.axis_index("gx"), lax.axis_index("gy")]).astype(jnp.int32)
    tm, tp = depth_table(nz, False), depth_table(nz, True)
    xedge, yedge = shape(3, R, ny, nz), shape(3, nx, R, nz)
    edges = (xedge, xedge, yedge, yedge)
    ext = (nx + 2 * OX, ny + 2 * OY, nz)
    vext, sext = shape(3, *ext), shape(6, *ext)
    dma = pltpu.SemaphoreType.DMA
    cost = pl.CostEstimate(flops=1 << 30, bytes_accessed=16 << 20, transcendentals=0)

    block = chan_block.reshape(1, count)
    requests = call(request_kernel, shape(devices, 4 * slots), [VM] * 4, VM)(
        block,
        chan_cell.reshape(1, count),
        jnp.cos(chan_azimuth).reshape(1, count),
        jnp.sin(chan_azimuth).reshape(1, count),
    )
    sent = call(
        pack_kernel, edges, [SM, HB], [VM] * 4,
        [pltpu.VMEM((3, nx, 8, nz), F32), pltpu.VMEM((3, nx, 8, nz), F32), dma((4,))],
    )(place, stress)
    halos = exchange(sent)
    asked = lax.all_to_all(requests, ("gx", "gy"), split_axis=0, concat_axis=0, tiled=True)
    asked, halos = lax.optimization_barrier((asked, halos))
    vel, strs, *sent = call(
        lambda *r: velocity_kernel(0, True, *r), (vext, sext, *edges),
        [SM] * 4 + [HB, HB] + [VM] * 7, [VM] * 6, [dma((2,))], cost=cost,
    )(place, src_x, src_y, src_amp, stress, velocity, material, tm, tp, *halos)
    halos = exchange(sent)
    vel, strs, *sent = call(
        lambda *r: stress_kernel(False, *r), (vext, sext, *edges),
        [SM] + [VM] * 9, [VM] * 6, aliases={1: 0, 2: 1}, cost=cost,
    )(place, vel, strs, material, tm, tp, *halos)
    halos = exchange(sent)
    vel, strs, *sent = call(
        lambda *r: velocity_kernel(1, False, *r), (vext, sext, *edges),
        [SM] * 4 + [VM] * 9, [VM] * 6, aliases={5: 0, 4: 1}, cost=cost,
    )(place, src_x, src_y, src_amp, strs, vel, material, tm, tp, *halos)
    halos = exchange(sent)
    picked = call(
        pick_kernel, shape(devices, 4 * slots), [SM, VM, VM], VM,
        [pltpu.VMEM((slots, devices, nz), F32)] * 2 + [pltpu.VMEM((devices + 8, 4 * slots), F32)],
    )(asked, asked, vel)
    back = lax.all_to_all(picked, ("gx", "gy"), split_axis=0, concat_axis=0, tiled=True)
    back, vel, strs, halos = lax.optimization_barrier((back, vel, strs, halos))
    _, velocity_out, stress_out = call(
        lambda *r: stress_kernel(True, *r), (vext, shape(3, nx, ny, nz), shape(6, nx, ny, nz)),
        [SM] + [VM] * 9, [VM, HB, HB], [pltpu.VMEM((6, nx, ny, nz), F32), dma((2,))],
        aliases={1: 0}, cost=cost,
    )(place, vel, strs, material, tm, tp, *halos)
    strain = call(strain_kernel, shape(1, count), [VM] * 3, VM)(block, gauge.reshape(1, count), back)
    return velocity_out, stress_out, strain.reshape(count)


def solution(mesh):
    grid, line = P(None, "gx", "gy", None), P(("gx", "gy"))
    return jax.shard_map(
        body,
        mesh=mesh,
        in_specs=(grid, grid, grid, P(), P(), P(), P(("gx", "gy"), None), line, line, line),
        out_specs=(grid, grid, line),
        check_vma=False,
    )
```

```python
import jax
import jax.numpy as jnp
import numpy as np
from jax import lax
from jax.experimental import pallas as pl
from jax.experimental.pallas import tpu as pltpu
from jax.sharding import PartitionSpec as P

STEPS = 2
COEFFS = (1225.0 / 1024.0, -245.0 / 3072.0, 49.0 / 5120.0, -5.0 / 7168.0)
RATIO = tuple(c / COEFFS[0] for c in COEFFS)
time_step = 0.2
SCALE = time_step * COEFFS[0]
R = 4
OX, OY = 4, 8
PLANES = 2

VM = pl.BlockSpec(memory_space=pltpu.VMEM)
SM = pl.BlockSpec(memory_space=pltpu.SMEM)
HB = pl.BlockSpec(memory_space=pltpu.HBM)
F32 = jnp.float32
BF16 = jnp.bfloat16


def shape(*dims):
    return jax.ShapeDtypeStruct(dims, F32)


def swap_pairs(count, first):
    route = []
    for i in range(first, count - 1, 2):
        route += [(i, i + 1), (i + 1, i)]
    return route


def depth_table(depth, forward):
    table = np.zeros((depth, depth), np.float64)
    for m in range(1, 5):
        up, down = (m, 1 - m) if forward else (m - 1, -m)
        for t in range(depth):
            if 0 <= t + up < depth:
                table[t + up, t] += RATIO[m - 1]
            if 0 <= t + down < depth:
                table[t + down, t] -= RATIO[m - 1]
    high = jnp.asarray(table, F32).astype(BF16)
    low = (jnp.asarray(table, F32) - high.astype(F32)).astype(BF16)
    row = jnp.concatenate([high, low], axis=1)
    return jnp.concatenate([row, row], axis=0)


def diff_x(ref, f, x, r0, n, forward):
    total = None
    for m in range(1, 5):
        up, down = (m, 1 - m) if forward else (m - 1, -m)
        term = ref[f, x + OX + up, OY + r0 : OY + r0 + n, :] - ref[f, x + OX + down, OY + r0 : OY + r0 + n, :]
        total = term if m == 1 else total + RATIO[m - 1] * term
    return total


def diff_y(ref, f, x, r0, n, forward):
    total = None
    for m in range(1, 5):
        up, down = (m, 1 - m) if forward else (m - 1, -m)
        a, b = OY + r0 + up, OY + r0 + down
        term = ref[f, x + OX, a : a + n, :] - ref[f, x + OX, b : b + n, :]
        total = term if m == 1 else total + RATIO[m - 1] * term
    return total


def diff_z(ref, fields, x, planes, ny, table):
    parts = []
    for f in fields:
        for p in range(planes):
            v = ref[f, x + p + OX, OY : OY + ny, :]
            high = v.astype(BF16)
            low = (v - high.astype(F32)).astype(BF16)
            parts.append(jnp.concatenate([high, low], axis=1))
    both = jnp.dot(jnp.concatenate(parts, axis=0), table, preferred_element_type=F32)
    depth = both.shape[1] // 2
    return both[:, :depth] + both[:, depth:]


def put_halos(ext, xf, yf, px, py, rxe, rxo, rye, ryo):
    nx, ny = ext.shape[1] - 2 * OX, ext.shape[2] - 2 * OY
    e, o = (OX + nx) * (1 - px), (OX + nx) * px
    for i, f in enumerate(xf):
        ext[f, pl.ds(e, R), OY : OY + ny, :] = rxe[i]
        ext[f, pl.ds(o, R), OY : OY + ny, :] = rxo[i]

    def rows(at_e, at_o):
        def step(x):
            for i, f in enumerate(yf):
                ext[f, x + OX, at_e : at_e + R, :] = rye[i, x]
                ext[f, x + OX, at_o : at_o + R, :] = ryo[i, x]

        unrolled(nx, step)

    pl.when(py == 0)(lambda: rows(OY + ny, OY - R))
    pl.when(py == 1)(lambda: rows(OY - R, OY + ny))


def take_edges(ext, xf, yf, px, py, sxe, sxo, sye, syo):
    nx, ny = ext.shape[1] - 2 * OX, ext.shape[2] - 2 * OY
    e, o = OX + (nx - R) * (1 - px), OX + (nx - R) * px
    for i, f in enumerate(xf):
        sxe[i] = ext[f, pl.ds(e, R), OY : OY + ny, :]
        sxo[i] = ext[f, pl.ds(o, R), OY : OY + ny, :]

    def rows(at_e, at_o):
        def step(x):
            for i, f in enumerate(yf):
                sye[i, x] = ext[f, x + OX, at_e : at_e + R, :]
                syo[i, x] = ext[f, x + OX, at_o : at_o + R, :]

        unrolled(nx, step)

    pl.when(py == 0)(lambda: rows(OY + ny - R, OY))
    pl.when(py == 1)(lambda: rows(OY, OY + ny - R))


def halo_terms(i, forward, low):
    found = []
    for m in range(1, 5):
        if low:
            at = i + (1 - m if forward else -m)
            if at < 0:
                found.append((R + at, -RATIO[m - 1]))
        else:
            at = (m if forward else m - 1) - i - 1
            if at >= 0:
                found.append((at, RATIO[m - 1]))
    return found


def weighted(layers, terms):
    total = None
    for layer, weight in terms:
        term = weight * layers(layer)
        total = term if total is None else total + term
    return total


def row_weights(forward, low, depth):
    row = lax.broadcasted_iota(jnp.int32, (8, depth), 0)
    tables = [jnp.zeros((8, depth), F32) for _ in range(R)]
    for i in range(R):
        for layer, weight in halo_terms(i, forward, low):
            tables[layer] = jnp.where(row == (i if low else 7 - i), weight, tables[layer])
    return tables


def clear_halos(ext, fields):
    nx, ny, depth = ext.shape[1] - 2 * OX, ext.shape[2] - 2 * OY, ext.shape[3]
    for f in fields:
        for x in (0, OX + nx):
            ext[f, x : x + R, OY : OY + ny, :] = jnp.zeros((R, ny, depth), F32)
        for y in (0, OY + ny):
            ext[f, OX : OX + nx, y : y + 8, :] = jnp.zeros((nx, 8, depth), F32)


def sides(p, re, ro):
    return lambda i, k, rows: jnp.where(p == 0, ro[i, k, rows], re[i, k, rows]), lambda i, k, rows: jnp.where(
        p == 0, re[i, k, rows], ro[i, k, rows]
    )


def unrolled(count, step):
    def block(j, carry):
        for k in range(4):
            step(j * 4 + k)
        return carry

    lax.fori_loop(0, count // 4, block, 0)


def pack_kernel(place, stress, *refs):
    small, refs = refs[:6], refs[6:]
    sxe, sxo, sye, syo, requests, force, tile_e, tile_o, *held, sems, small_sems = refs
    loads = [pltpu.make_async_copy(a, b, small_sems.at[i]) for i, (a, b) in enumerate(zip(small, held))]
    for c in loads:
        c.start()
    src_x, src_y, amp, block_ref, cell_ref, azimuth = held
    nx, ny, nz = stress.shape[1:]
    px, py = place[0] % 2, place[1] % 2
    e, o = (nx - R) * (1 - px), (nx - R) * px
    te, to = pl.multiple_of((ny - 8) * (1 - py), 8), pl.multiple_of((ny - 8) * py, 8)
    copies = [
        pltpu.make_async_copy(stress.at[2:5, :, pl.ds(te, 8), :], tile_e, sems.at[0]),
        pltpu.make_async_copy(stress.at[2:5, :, pl.ds(to, 8), :], tile_o, sems.at[1]),
        pltpu.make_async_copy(stress.at[0:3, pl.ds(e, R)], sxe, sems.at[2]),
        pltpu.make_async_copy(stress.at[0:3, pl.ds(o, R)], sxo, sems.at[3]),
    ]
    for c in copies:
        c.start()

    for c in loads:
        c.wait()
    sources = amp.shape[1]
    row = lax.broadcasted_iota(jnp.int32, (ny, sources), 0) + place[1] * ny
    lane = lax.broadcasted_iota(jnp.int32, (nz, sources), 0)
    for s in range(amp.shape[0]):
        hit_y = jnp.where(row == src_y[s : s + 1, :], 1.0, 0.0)
        hit_x = (lane == src_x[s : s + 1, :] - place[0] * nx) & (lane < nx)
        hit_x = jnp.where(hit_x, amp[s : s + 1, :] * (1.0 / COEFFS[0]), 0.0)
        force[s] = lax.dot_general(
            hit_y, hit_x, (((1,), (1,)), ((), ())),
            precision=lax.Precision.HIGHEST, preferred_element_type=F32,
        )
    make_requests(ny, nz, block_ref, cell_ref, azimuth, requests)
    copies[0].wait()
    copies[1].wait()

    def rows(at_e, at_o):
        def step(x):
            for i in range(3):
                sye[i, x] = tile_e[i, x, at_e : at_e + R, :]
                syo[i, x] = tile_o[i, x, at_o : at_o + R, :]

        unrolled(nx, step)

    pl.when(py == 0)(lambda: rows(8 - R, 0))
    pl.when(py == 1)(lambda: rows(0, 8 - R))
    copies[2].wait()
    copies[3].wait()


def velocity_planes(x0, step, se, ve, mat, force, tm, tp):
    ny, depth = ve.shape[2] - 2 * OY, ve.shape[3]
    zm = diff_z(se, (1, 3), x0, PLANES, ny, tm[...])
    zp = diff_z(se, (5,), x0, PLANES, ny, tp[...])
    n = 16
    surface = lax.broadcasted_iota(jnp.int32, (n, depth), 1) == 0
    for p in range(PLANES):
        x = x0 + p
        push = pltpu.roll(force[step], (depth - x) % depth, 1)
        for r0 in range(0, ny, n):
            a, b = p * ny + r0, (PLANES + p) * ny + r0
            here = (slice(OY + r0, OY + r0 + n), slice(None))
            sb = SCALE * mat[2, x, r0 : r0 + n, :]
            rate = diff_x(se, 0, x, r0, n, True) + diff_y(se, 2, x, r0, n, False) + zm[a : a + n]
            ve[(0, x + OX, *here)] = ve[(0, x + OX, *here)] + sb * rate
            rate = diff_x(se, 2, x, r0, n, False) + diff_y(se, 4, x, r0, n, True) + zm[b : b + n]
            ve[(1, x + OX, *here)] = ve[(1, x + OX, *here)] + sb * rate
            rate = diff_x(se, 1, x, r0, n, False) + diff_y(se, 3, x, r0, n, False) + zp[a : a + n]
            rate = rate + jnp.where(surface, push[r0 : r0 + n], 0.0)
            ve[(2, x + OX, *here)] = ve[(2, x + OX, *here)] + sb * rate


def first_velocity_kernel(place, force, stress, vel, mat, tm, tp, rxe, rxo, rye, ryo,
                          ve, se, sxe, sxo, sye, syo, sem_s, sem_v):
    nx, ny = stress.shape[1], stress.shape[2]
    chunks = nx // R

    def load(src, dst, sems, j):
        planes = pl.ds(OX + j * R, R)
        return pltpu.make_async_copy(src.at[:, pl.ds(j * R, R)], dst.at[:, planes, OY : OY + ny, :], sems.at[j])

    for j in range(chunks):
        load(stress, se, sem_s, j).start()
        load(vel, ve, sem_v, j).start()
    px, py = place[0] % 2, place[1] % 2
    put_halos(se, (0, 1, 2), (2, 3, 4), px, py, rxe, rxo, rye, ryo)
    load(stress, se, sem_s, 0).wait()

    def chunk(j, carry):
        @pl.when(j + 1 < chunks)
        def _():
            load(stress, se, sem_s, j + 1).wait()

        load(vel, ve, sem_v, j).wait()

        def planes(k, inner):
            velocity_planes(j * R + k * PLANES, 0, se, ve, mat, force, tm, tp)
            return inner

        return lax.fori_loop(0, R // PLANES, planes, carry)

    lax.fori_loop(0, chunks, chunk, 0)
    take_edges(ve, (0, 1, 2), (0, 1, 2), px, py, sxe, sxo, sye, syo)


def velocity_bulk_kernel(step, force, ve_in, se_in, mat, tm, tp, ve, se):
    clear_halos(se, range(5))

    def planes(k, carry):
        velocity_planes(k * PLANES, step, se, ve, mat, force, tm, tp)
        return carry

    lax.fori_loop(0, (se.shape[1] - 2 * OX) // PLANES, planes, 0)


def velocity_edge_kernel(place, ve_in, mat, rxe, rxo, rye, ryo, ve, sxe, sxo, sye, syo):
    nx, ny, depth = ve.shape[1] - 2 * OX, ve.shape[2] - 2 * OY, ve.shape[3]
    px, py = place[0] % 2, place[1] % 2
    every = slice(None)
    halo_x, halo_y = sides(px, rxe, rxo), sides(py, rye, ryo)
    for low in (True, False):
        for i in range(R):
            x = i if low else nx - 1 - i
            for r0 in range(0, ny, 32):
                part = slice(r0, r0 + 32)
                sb = SCALE * mat[2, x, part, :]
                for c, f, forward in ((0, 0, True), (1, 2, False), (2, 1, False)):
                    terms = halo_terms(i, forward, low)
                    if terms:
                        rate = weighted(lambda k: halo_x[0 if low else 1](f, k, part), terms)
                        here = (c, x + OX, slice(OY + r0, OY + r0 + 32), every)
                        ve[here] = ve[here] + sb * rate
    tables = {(w, low): row_weights(w, low, depth) for w in (True, False) for low in (True, False)}

    def step(x):
        for low in (True, False):
            r0 = 0 if low else ny - 8
            sb = SCALE * mat[2, x, r0 : r0 + 8, :]
            for c, f, forward in ((0, 0, False), (1, 2, True), (2, 1, False)):
                rate = None
                for k in range(R):
                    term = tables[forward, low][k] * halo_y[0 if low else 1](f, x, slice(k, k + 1))
                    rate = term if rate is None else rate + term
                here = (c, x + OX, slice(OY + r0, OY + r0 + 8), every)
                ve[here] = ve[here] + sb * rate

    unrolled(nx, step)
    take_edges(ve, (0, 1, 2), (0, 1, 2), px, py, sxe, sxo, sye, syo)


def stress_planes(x0, ve, se, mat, tm, tp, snew, ox, oy):
    ny = ve.shape[2] - 2 * OY
    zp = diff_z(ve, (0, 1), x0, PLANES, ny, tp[...])
    zm = diff_z(ve, (2,), x0, PLANES, ny, tm[...])
    n = 16
    for p in range(PLANES):
        x = x0 + p
        for r0 in range(0, ny, n):
            a, b = p * ny + r0, (PLANES + p) * ny + r0

            def add(f, change):
                snew[f, x + ox, oy + r0 : oy + r0 + n, :] = (
                    se[f, x + OX, OY + r0 : OY + r0 + n, :] + change
                )

            exx = diff_x(ve, 0, x, r0, n, False)
            eyy = diff_y(ve, 1, x, r0, n, False)
            ezz = zm[a : a + n]
            trace = (SCALE * mat[0, x, r0 : r0 + n, :]) * (exx + eyy + ezz)
            smu = SCALE * mat[1, x, r0 : r0 + n, :]
            twice = 2.0 * smu
            add(0, trace + twice * exx)
            add(4, trace + twice * eyy)
            add(5, trace + twice * ezz)
            add(2, smu * (diff_y(ve, 0, x, r0, n, True) + diff_x(ve, 1, x, r0, n, True)))
            add(1, smu * (zp[a : a + n] + diff_x(ve, 2, x, r0, n, True)))
            add(3, smu * (zp[b : b + n] + diff_y(ve, 2, x, r0, n, True)))


def stress_bulk_kernel(ve_in, se_in, mat, tm, tp, ve, se):
    clear_halos(ve, range(3))

    def planes(k, carry):
        stress_planes(k * PLANES, ve, se, mat, tm, tp, se, OX, OY)
        return carry

    lax.fori_loop(0, (ve.shape[1] - 2 * OX) // PLANES, planes, 0)


def stress_edge_kernel(place, se_in, mat, rxe, rxo, rye, ryo, se, sxe, sxo, sye, syo):
    nx, ny, depth = se.shape[1] - 2 * OX, se.shape[2] - 2 * OY, se.shape[3]
    px, py = place[0] % 2, place[1] % 2
    every = slice(None)
    halo_x, halo_y = sides(px, rxe, rxo), sides(py, rye, ryo)

    def spread(x, r0, n, normal, own, shears):
        inside = (x + OX, slice(OY + r0, OY + r0 + n), every)
        smu = SCALE * mat[1, x, r0 : r0 + n, :]
        if normal is not None:
            trace = (SCALE * mat[0, x, r0 : r0 + n, :]) * normal
            for f in (0, 4, 5):
                change = trace + (2.0 * smu) * normal if f == own else trace
                se[(f, *inside)] = se[(f, *inside)] + change
        for f, change in shears:
            if change is not None:
                se[(f, *inside)] = se[(f, *inside)] + smu * change

    for low in (True, False):
        for i in range(R):
            x = i if low else nx - 1 - i
            for r0 in range(0, ny, 32):
                part = slice(r0, r0 + 32)

                def of(c, forward):
                    return weighted(lambda k: halo_x[0 if low else 1](c, k, part), halo_terms(i, forward, low))

                spread(x, r0, 32, of(0, False), 0, ((2, of(1, True)), (1, of(2, True))))
    tables = {(w, low): row_weights(w, low, depth) for w in (True, False) for low in (True, False)}

    def step(x):
        for low in (True, False):

            def of(c, forward):
                total = None
                for k in range(R):
                    term = tables[forward, low][k] * halo_y[0 if low else 1](c, x, slice(k, k + 1))
                    total = term if total is None else total + term
                return total

            spread(x, 0 if low else ny - 8, 8, of(1, False), 4, ((2, of(0, True)), (3, of(2, True))))

    unrolled(nx, step)
    take_edges(se, (0, 1, 2), (2, 3, 4), px, py, sxe, sxo, sye, syo)


def last_stress_kernel(place, ve_in, se, mat, tm, tp, rxe, rxo, rye, ryo, ve, vout, sout, snew, sems):
    nx, ny = ve.shape[1] - 2 * OX, ve.shape[2] - 2 * OY
    inner = (slice(None), slice(OX, OX + nx), slice(OY, OY + ny), slice(None))
    vcopy = pltpu.make_async_copy(ve.at[inner], vout, sems.at[0])
    vcopy.start()
    put_halos(ve, (0, 1, 2), (0, 1, 2), place[0] % 2, place[1] % 2, rxe, rxo, rye, ryo)

    def planes(k, carry):
        stress_planes(k * PLANES, ve, se, mat, tm, tp, snew, 0, 0)
        at = pl.ds(k * PLANES, PLANES)
        pltpu.make_async_copy(snew.at[:, at], sout.at[:, at], sems.at[1]).start()
        return carry

    lax.fori_loop(0, nx // PLANES, planes, 0)
    pltpu.make_async_copy(snew, sout, sems.at[1]).wait()
    vcopy.wait()


def to_column(row, i, width):
    eye = lax.broadcasted_iota(jnp.int32, (width, width), 0) == lax.broadcasted_iota(
        jnp.int32, (width, width), 1
    )
    part = jnp.broadcast_to(row[:, i * width : (i + 1) * width], (width, width))
    return jnp.sum(jnp.where(eye, part, 0.0), axis=1, keepdims=True)


def ranks(block):
    count = block.shape[1]
    later = lax.broadcasted_iota(jnp.int32, (128, count), 1)
    total = jnp.zeros((1, count), F32)
    for i in range(count // 128):
        earlier = lax.broadcasted_iota(jnp.int32, (128, count), 0) + i * 128
        same = (to_column(block, i, 128) == block) & (earlier < later)
        total = total + jnp.sum(jnp.where(same, 1.0, 0.0), axis=0, keepdims=True)
    return total


def members(block, devices):
    owner = lax.broadcasted_iota(jnp.int32, (devices, block.shape[1]), 0).astype(F32)
    return jnp.where(owner == block, 1.0, 0.0)


def make_requests(ny, depth, block_ref, cell_ref, azimuth, out):
    devices, slots = out.shape[0], out.shape[1] // 5
    block = block_ref[...].astype(F32)
    rank = ranks(block)
    cell = cell_ref[...]
    x, y, z = lax.div(cell, ny * depth), lax.rem(lax.div(cell, depth), ny), lax.rem(cell, depth)
    row = (x + OX) * (ny + 2 * OY) + y + OY
    place = lax.broadcasted_iota(jnp.int32, block.shape, 1) + 1
    angle = azimuth[...]
    rows = []
    for value in (row.astype(F32), z.astype(F32), jnp.cos(angle), jnp.sin(angle), place.astype(F32)):
        for r in range(slots):
            rows.append(jnp.where(rank == float(r), value, 0.0))
    out[...] = lax.dot_general(
        members(block, devices),
        jnp.concatenate(rows, axis=0),
        (((1,), (1,)), ((), ())),
        precision=lax.Precision.HIGHEST,
        preferred_element_type=F32,
    )


def pick_kernel(asked, ve, out, rows_x, rows_y, ahead, wanted, want, sem):
    devices, slots = asked.shape[0], asked.shape[1] // 5
    depth, plane = ve.shape[1], ve.shape[0] // 3
    asks = asked[...]
    wanted[:, 0 : asks.shape[1]] = asks.astype(jnp.int32)
    copy = pltpu.make_async_copy(wanted, want, sem)
    copy.start()
    copy.wait()

    def fetch(j, carry):
        for k in range(8):
            for r in range(slots):
                row = want[j * 8 + k, r]
                rows_x[r, pl.ds(j * 8 + k, 1), :] = ve[pl.ds(row, 1), :]
                rows_y[r, pl.ds(j * 8 + k, 1), :] = ve[pl.ds(row + plane, 1), :]
        return carry

    lax.fori_loop(0, devices // 8, fetch, 0)
    lane = lax.broadcasted_iota(jnp.int32, (devices, depth), 1).astype(F32)
    column = lax.broadcasted_iota(jnp.int32, asks.shape, 1)
    picked = jnp.zeros(asks.shape, F32)
    for r in range(slots):
        row, z, cosine, sine = (asks[:, q * slots + r : q * slots + r + 1] for q in range(4))
        hit = (row > 0.0) & (lane == z)
        value = jnp.sum(jnp.where(hit, cosine * rows_x[r] + sine * rows_y[r], 0.0), axis=1, keepdims=True)
        picked = jnp.where(column == r, value, picked)
    ahead[devices : devices + 8, :] = jnp.zeros((8, asks.shape[1]), F32)
    ahead[0:devices, :] = jnp.where(column >= 4 * slots, asks, picked)
    nxt = ahead[1 : devices + 1, :]
    for r in range(slots):
        picked = jnp.where(column == slots + r, nxt[:, r : r + 1], picked)
    out[...] = jnp.where(column < 2 * slots, picked, nxt)


def strain_kernel(block_ref, gauge_ref, back_ref, out):
    devices, slots = back_ref.shape[0], back_ref.shape[1] // 5
    count = block_ref.shape[1]
    block, gauge = block_ref[...].astype(F32), gauge_ref[...]
    back = back_ref[...]
    rank = ranks(block)
    mine = lax.dot_general(
        back,
        members(block, devices),
        (((0,), (0,)), ((), ())),
        precision=lax.Precision.HIGHEST,
        preferred_element_type=F32,
    )
    along = jnp.zeros((1, count), F32)
    for r in range(slots):
        along = along + jnp.where(rank == float(r), mine[r : r + 1, :], 0.0)
    place = lax.broadcasted_iota(jnp.int32, (devices, 128), 1).astype(F32) + 1.0
    following = jnp.zeros((1, 128), F32)
    for r in range(slots):
        hit = back[:, 4 * slots + r : 4 * slots + r + 1] == place
        following = following + jnp.sum(
            jnp.where(hit, back[:, slots + r : slots + r + 1], 0.0), axis=0, keepdims=True
        )
    goal = lax.broadcasted_iota(jnp.int32, (128, count), 1) + gauge
    ahead = jnp.zeros((1, count), F32)
    for i in range(count // 128 + 1):
        values = to_column(along, i, 128) if i < count // 128 else to_column(following, 0, 128)
        source = lax.broadcasted_iota(jnp.int32, (128, count), 0) + i * 128
        ahead = ahead + jnp.sum(jnp.where(source == goal, values, 0.0), axis=0, keepdims=True)
    out[...] = (ahead - along) / gauge.astype(F32)


def call(kernel, outs, in_specs, out_specs, scratch=(), aliases=None, cost=None, mib=8):
    return pl.pallas_call(
        kernel,
        out_shape=outs,
        in_specs=in_specs,
        out_specs=out_specs,
        scratch_shapes=list(scratch),
        input_output_aliases=aliases or {},
        compiler_params=pltpu.CompilerParams(vmem_limit_bytes=mib << 20),
        cost_estimate=cost,
    )


def exchange(edges):
    sxe, sxo, sye, syo = edges
    ngx, ngy = lax.axis_size("gx"), lax.axis_size("gy")
    ryo = lax.ppermute(syo, "gy", swap_pairs(ngy, 1))
    rxo = lax.ppermute(sxo, "gx", swap_pairs(ngx, 1))
    rye = lax.ppermute(sye, "gy", swap_pairs(ngy, 0))
    rxe = lax.ppermute(sxe, "gx", swap_pairs(ngx, 0))
    return rxe, rxo, rye, ryo


def body(velocity, stress, material, src_x, src_y, src_amp, chan_block, chan_cell, chan_azimuth, gauge):
    _, nx, ny, nz = material.shape
    devices = lax.axis_size("gx") * lax.axis_size("gy")
    count = chan_cell.shape[0]
    slots = 4
    place = jnp.stack([lax.axis_index("gx"), lax.axis_index("gy")]).astype(jnp.int32)
    tm, tp = depth_table(nz, False), depth_table(nz, True)
    xedge, yedge = shape(3, R, ny, nz), shape(3, nx, R, nz)
    edges = (xedge, xedge, yedge, yedge)
    ext = (nx + 2 * OX, ny + 2 * OY, nz)
    vext, sext = shape(3, *ext), shape(6, *ext)
    dma = pltpu.SemaphoreType.DMA
    cost = pl.CostEstimate(flops=1 << 30, bytes_accessed=16 << 20, transcendentals=0)

    block = chan_block.reshape(1, count)
    width = 5 * slots
    stress_hbm = pltpu.with_memory_space_constraint(stress, pltpu.HBM)
    velocity_hbm = pltpu.with_memory_space_constraint(velocity, pltpu.HBM)
    tile = pltpu.VMEM((3, nx, 8, nz), F32)
    small = (src_x, src_y, src_amp, block, chan_cell.reshape(1, count), chan_azimuth.reshape(1, count))
    *sent, requests, force = call(
        pack_kernel, (*edges, shape(devices, width), shape(STEPS, ny, nz)),
        [SM] + [HB] * 7, [VM] * 6,
        [tile, tile, *(pltpu.VMEM(a.shape, a.dtype) for a in small), dma((4,)), dma((6,))],
    )(place, stress_hbm, *(pltpu.with_memory_space_constraint(a, pltpu.HBM) for a in small))
    halos = exchange(sent)
    asked = lax.all_to_all(requests, ("gx", "gy"), split_axis=0, concat_axis=0, tiled=True)
    asked, halos = lax.optimization_barrier((asked, halos))
    vel, strs, *sent = call(
        first_velocity_kernel, (vext, sext, *edges),
        [SM, VM, HB, HB] + [VM] * 7, [VM] * 6, [dma((nx // R,)), dma((nx // R,))], cost=cost,
    )(place, force, stress_hbm, velocity_hbm, material, tm, tp, *halos)

    halos = exchange(sent)
    vel, strs = call(
        stress_bulk_kernel, (vext, sext), [VM] * 5, [VM] * 2, aliases={0: 0, 1: 1}, cost=cost,
    )(vel, strs, material, tm, tp)
    strs, *sent = call(
        stress_edge_kernel, (sext, *edges), [SM] + [VM] * 6, [VM] * 5, aliases={1: 0},
    )(place, strs, material, *halos)

    halos = exchange(sent)
    vel, strs = call(
        lambda *r: velocity_bulk_kernel(1, *r), (vext, sext), [VM] * 6, [VM] * 2,
        aliases={1: 0, 2: 1}, cost=cost,
    )(force, vel, strs, material, tm, tp)
    vel, *sent = call(
        velocity_edge_kernel, (vext, *edges), [SM] + [VM] * 6, [VM] * 5, aliases={1: 0},
    )(place, vel, material, *halos)

    halos = exchange(sent)
    flat = vel.reshape(3 * ext[0] * ext[1], nz)
    picked = call(
        pick_kernel, shape(devices, width), [VM, VM], VM,
        [pltpu.VMEM((slots, devices, nz), F32)] * 2
        + [pltpu.VMEM((devices + 8, width), F32), pltpu.VMEM((devices, 128), jnp.int32),
           pltpu.SMEM((devices, 128), jnp.int32), dma],
    )(asked, flat)
    back = lax.all_to_all(picked, ("gx", "gy"), split_axis=0, concat_axis=0, tiled=True)
    back, vel, strs, halos = lax.optimization_barrier((back, vel, strs, halos))
    _, velocity_out, stress_out = call(
        last_stress_kernel, (vext, shape(3, nx, ny, nz), shape(6, nx, ny, nz)),
        [SM] + [VM] * 9, [VM, HB, HB], [pltpu.VMEM((6, nx, ny, nz), F32), dma((2,))],
        aliases={1: 0}, cost=cost,
    )(place, vel, strs, material, tm, tp, *halos)
    strain = call(strain_kernel, shape(1, count), [VM] * 3, VM)(block, gauge.reshape(1, count), back)
    return velocity_out, stress_out, strain.reshape(count)


def solution(mesh):
    grid, line = P(None, "gx", "gy", None), P(("gx", "gy"))
    return jax.shard_map(
        body,
        mesh=mesh,
        in_specs=(grid, grid, grid, P(), P(), P(), P(("gx", "gy"), None), line, line, line),
        out_specs=(grid, grid, line),
        check_vma=False,
    )
```
